32 devices in a mesh: groups: 2 (over y), pair: 4 (over z), virt: 2 (over x), sub: 2 (over core).
Axes of the slice: x: 2, y: 2, z: 4, core: 2. Of those that a mesh axis runs over, the one named last changes fastest.
Arguments:
- amplitudes: bfloat16 [512, 256], P(('groups', 'pair'), ('virt', 'sub')), parts along dimension 0, may hold values from -6 to 6
- integrals: bfloat16 [256, 14400], P(('pair', 'sub'), 'virt'), may hold values from -0.375 to 0.375
- mirror: int32 [256], replicated, may hold values from 0 to 255, as said below
Outputs:
- ladder: bfloat16 [512, 14400], P(('groups', 'pair'), ('virt', 'sub')), parts along dimension 0
The draws below stay inside these ranges and needn't reach their ends.
There are 2 independent parts, one for each index of `groups`. The reference program is written for one: setup_inputs(seed, part) draws one part's arguments, and reference() takes and returns one part's arrays. A program takes and returns all parts, laid end to end along the dimension named above; an argument that names none is the same for every part. Nothing has to cross between parts.
Inputs may be any that keep to these rules, and one draw needn't show every extreme that they name: mirror is an involution without fixed points: mirror[mirror[k]] = k and mirror[k] != k.
All inputs are finite; a program needn't handle non-finite values.
Results may differ from the reference program's by a relative error of at most 0.0051.
Values may be sent and summed in bfloat16 or wider, within the bound.
No kernel may reach another device: no remote copies, remote signals or barrier semaphores. Data moves between devices by JAX's collectives and lax.ppermute only.
A program may use at most 64 MiB of HBM per device.

```python
import jax
import jax.numpy as jnp

P_SIZE = 256
CD = 256
AB = 14400


def draw_mirror(key, part):
    order = jax.random.permutation(key, CD).astype(jnp.int32)
    first = order[0::2]
    second = order[1::2]
    result = jnp.zeros((CD,), jnp.int32).at[first].set(second).at[second].set(first)
    return result


def levels(stream_key, dims, shards, smallest, high):
    gain, own = 1.0, jax.random.fold_in(stream_key, 6)
    for axis_at, shards_of in shards:
        draws = jnp.exp(jax.random.uniform(jax.random.fold_in(own, axis_at), (shards_of,), jnp.float32, smallest / len(shards), high / len(shards)))
        gain = gain * jnp.repeat(draws, dims[axis_at] // shards_of).reshape([-1 if axis == axis_at else 1 for axis in range(len(dims))])
    return gain


def normal_values(key, dims, spread, limit, cuts=(), dtype=jnp.bfloat16):
    level = levels(key, dims, cuts, -0.22, 0.18) if cuts else 1.0
    drawn = jax.random.normal(key, dims, jnp.float32) * spread * level
    return jnp.minimum(jnp.maximum(drawn, -limit), limit).astype(dtype)


def setup_inputs(seed: int = 0, part: int = 0) -> dict:
    splits = jax.random.split(jax.random.key(seed), 4)
    part_keys = jax.random.split(jax.random.fold_in(splits[3], part), 4)
    return {
        "amplitudes": normal_values(part_keys[0], (P_SIZE, CD), 1.0, 6.0, ((0, 4), (1, 4))),
        "integrals": normal_values(splits[1], (CD, AB), CD ** -0.5, 0.375, ((0, 8), (1, 2))),
        "mirror": draw_mirror(jax.random.fold_in(splits[3], 71), part),
    }


def reference(amplitudes, integrals, mirror):
    widened = amplitudes.astype(jnp.float32)
    antisym = (widened - jnp.take(widened, mirror, axis=1)).astype(jnp.bfloat16)
    result = jnp.dot(antisym, integrals, preferred_element_type=jnp.float32)
    return result.astype(jnp.bfloat16)
```

```python
import jax
import jax.numpy as jnp
from jax import lax
from jax.sharding import PartitionSpec as P

LANE = 128
CHUNKS = 1


def solution(mesh):
    n_pair, n_virt, n_sub = mesh.shape["pair"], mesh.shape["virt"], mesh.shape["sub"]
    n_groups = mesh.shape["groups"]

    def swap(value, axis, step):
        size = mesh.shape[axis]
        return lax.ppermute(value, axis, [(i, i ^ step) for i in range(size)])

    def body(amplitudes, integrals, mirror):
        core = lax.axis_index("sub")
        group = lax.axis_index("groups")
        me = lax.axis_index("pair")
        virt = lax.axis_index("virt")
        rows, wide = integrals.shape
        half = wide // n_sub
        start = half // LANE * LANE
        width = wide - start
        cuts = [round(width * i / CHUNKS / LANE) * LANE for i in range(CHUNKS)] + [width]

        pieces = []
        for lo, hi in zip(cuts[:-1], cuts[1:]):
            low = integrals[:, lo:hi]
            high = integrals[:, start + lo : start + hi]
            keep = jnp.where(core == 0, low, high)
            give = jnp.where(core == 0, high, low)
            got = swap(give, "sub", 1)
            mine = jnp.where(core == group, keep, got)
            other = jnp.where(core == group, got, keep)
            pieces.append((mine, other))

        held = [{0: m} for m, _ in pieces]
        step = n_pair // 2
        while step:
            for h in held:
                for d in list(h):
                    h[d ^ step] = swap(h[d], "pair", step)
            step //= 2
        theirs = [{d: (o if d == 0 else swap(h[d], "groups", 1)) for d in h} for h, (_, o) in zip(held, pieces)]

        slab = amplitudes.shape[1]
        blocks, bases = [amplitudes], [virt * n_sub + core]
        blocks.append(swap(amplitudes, "sub", 1)); bases.append(virt * n_sub + (1 - core))
        both = jnp.concatenate(blocks, axis=1)
        groups_of = [(both, virt)]
        for d in range(1, n_virt):
            groups_of.append((swap(both, "virt", d), virt ^ d))
        amps = jnp.concatenate([g for g, _ in groups_of], axis=1)
        k_of = jnp.concatenate([(v * n_sub + c) * slab + jnp.arange(slab) for _, v in groups_of for c in (core, 1 - core)])
        order = [(d, s) for d in held[0] for s in (0, 1)]
        slot_k = jnp.concatenate([((me ^ d) * n_sub + jnp.where(s == 0, group, 1 - group)) * rows + jnp.arange(rows) for d, s in order])
        slot_m = mirror[slot_k]
        pick = (k_of[:, None] == slot_k[None, :]).astype(jnp.bfloat16) - (k_of[:, None] == slot_m[None, :]).astype(jnp.bfloat16)
        antisym = jnp.dot(amps, pick, preferred_element_type=jnp.float32).astype(jnp.bfloat16)

        outs = []
        for h, t in zip(held, theirs):
            total = None
            for i, (d, s) in enumerate(order):
                term = jnp.dot(antisym[:, i * rows : (i + 1) * rows], (h if s == 0 else t)[d], preferred_element_type=jnp.float32)
                total = term if total is None else total + term
            outs.append(total.astype(jnp.bfloat16))
        full = jnp.concatenate(outs, axis=1) if len(outs) > 1 else outs[0]
        skew = half - start
        return jnp.where(core == 0, full[:, :half], full[:, skew : skew + half])

    return jax.shard_map(
        body,
        mesh=mesh,
        in_specs=(P(("groups", "pair"), ("virt", "sub")), P(("pair", "sub"), "virt"), P()),
        out_specs=P(("groups", "pair"), ("virt", "sub")),
        check_vma=False,
    )
```
